768 devices in a mesh: gx: 64 (over y, z_hi, core), gy: 12 (over z_lo, x).
Axes of the slice: x: 4, y: 8, z: 12 (z_hi: 4, z_lo: 3; z = z_hi * 3 + z_lo), core: 2. Of those that a mesh axis runs over, the one named last changes fastest.
Arguments:
- state: float32 [9, 56, 98304], P(None, None, ('gx', 'gy')), may hold values from -6 to 6
- star_matrices: float32 [3, 9, 9, 98304], P(None, None, None, ('gx', 'gy')), may hold values from -1.25 to 1.25
- stiffness: float32 [3, 56, 56], replicated, may hold values from -0.75 to 0.75
- face_project: float32 [4, 21, 56], replicated, may hold values from -0.75 to 0.75
- flux_inner: float32 [9, 9], replicated, may hold values from -2 to 2
- flux_outer: float32 [9, 9], replicated, may hold values from -2 to 2
- rate_level: int32 [98304], P(('gx', 'gy')), may hold values from 0 to 2
- neighbour: int32 [4, 98304], P(None, ('gx', 'gy')), may hold values from 0 to 511
- send_slots: int32 [4, 196608], P(None, ('gx', 'gy')), may hold values from 0 to 511
- receive_slots: int32 [4, 196608], P(None, ('gx', 'gy')), may hold values from 0 to 511
- fault_faces: int32 [49152], P(('gx', 'gy')), may hold values from 0 to 511, as said below
- slip_flags: int32 [49152], P(('gx', 'gy')), may hold values 0 or 1
Outputs:
- updated: float32 [9, 56, 98304], P(None, None, ('gx', 'gy'))
The draws below stay inside these ranges and needn't reach their ends.
Inputs may be any that keep to these rules, and one draw needn't show every extreme that they name: `neighbour`: local face indices f * 128 + e of the device's own elements. `send_slots`: local face indices of the sending device's own elements. `receive_slots`: local face indices of the receiving device's own elements; two slots may act on one face. `fault_faces`: local face indices of the device's own elements, distinct within one device.
All inputs are finite; a program needn't handle non-finite values. No bound on the sum of `slip_flags` on one device may be relied on, other than what follows from the above.
Results may differ from the reference program's by a relative error of at most 0.0003.
Values sent between devices are 32-bit elements; how exact they have to be, the bound alone decides.
No kernel may reach another device: no remote copies, remote signals or barrier semaphores. Data moves between devices by JAX's collectives and lax.ppermute only.
A program may use at most 64 MiB of HBM per device.

```python
import jax
import jax.numpy as jnp
from jax import lax

FIELDS = 9
MODES = 56
FACE_MODES = 21
ORDER = 6
E_DEV = 128
F_NB = 256
FAULT_DEV = 64
ELEMS = 98304
SLOTS = 196608
FAULTS = 49152
N_GX = 64
N_GY = 12


def draw_fault_faces(key, part):
    count = FAULTS // FAULT_DEV
    keys = jax.random.split(jax.random.fold_in(key, 7), count)

    def one_device(single):
        return jax.random.permutation(single, 4 * E_DEV)[:FAULT_DEV].astype(jnp.int32)
    return jax.vmap(one_device)(keys).reshape(FAULTS)


def plant(values, key, least, largest):
    index_at = [jax.random.randint(jax.random.fold_in(key, axis), (), 0, length) for axis, length in enumerate(values.shape)]
    main_axis = values.shape.index(max(values.shape))
    next_to = index_at[:main_axis] + [(index_at[main_axis] + 1) % values.shape[main_axis]] + index_at[main_axis + 1:]
    return values.at[tuple(index_at)].set(least).at[tuple(next_to)].set(largest)


def shard_levels(own_key, dims, shards, smallest, largest):
    def one(position, parts):
        draws = jax.random.uniform(jax.random.fold_in(jax.random.fold_in(own_key, 6), position), (parts,), jnp.float32, smallest / len(shards), largest / len(shards))
        return jnp.repeat(jnp.exp(draws), dims[position] // parts).reshape((-1,) + (1,) * (len(dims) - position - 1))

    factor_of = one(*shards[0])
    for cut in shards[1:]:
        factor_of = factor_of * one(*cut)
    return factor_of


def scatter_about(key, dims, deviation, bound, cuts=(), held_as=jnp.bfloat16):
    gain = shard_levels(key, dims, cuts, -0.22, 0.18) if cuts else 1.0
    result = jax.random.normal(key, dims, jnp.float32) * deviation * gain
    return jnp.minimum(jnp.maximum(result, -bound), bound).astype(held_as)


def setup_inputs(seed: int = 0) -> dict:
    key_of = jax.random.split(jax.random.key(seed), 13)
    return {
        "state": scatter_about(key_of[0], (FIELDS, MODES, ELEMS), 1.0, 6.0, ((2, 768),), jnp.float32),
        "star_matrices": scatter_about(key_of[1], (3, FIELDS, FIELDS, ELEMS), (3 * FIELDS) ** -0.5, 1.25, ((3, 768),), jnp.float32),
        "stiffness": scatter_about(key_of[2], (3, MODES, MODES), MODES ** -0.5, 0.75, (), jnp.float32),
        "face_project": scatter_about(key_of[3], (4, FACE_MODES, MODES), MODES ** -0.5, 0.75, (), jnp.float32),
        "flux_inner": scatter_about(key_of[4], (FIELDS, FIELDS), FIELDS ** -0.5, 2.0, (), jnp.float32),
        "flux_outer": scatter_about(key_of[5], (FIELDS, FIELDS), FIELDS ** -0.5, 2.0, (), jnp.float32),
        "rate_level": plant(jax.random.randint(key_of[6], (ELEMS,), 0, 3), jax.random.fold_in(key_of[6], 1), 0, 2).astype(jnp.int32),
        "neighbour": plant(jax.random.randint(key_of[7], (4, ELEMS), 0, 4 * E_DEV), jax.random.fold_in(key_of[7], 1), 0, (4 * E_DEV) - 1).astype(jnp.int32),
        "send_slots": plant(jax.random.randint(key_of[8], (4, SLOTS), 0, 4 * E_DEV), jax.random.fold_in(key_of[8], 1), 0, (4 * E_DEV) - 1).astype(jnp.int32),
        "receive_slots": plant(jax.random.randint(key_of[9], (4, SLOTS), 0, 4 * E_DEV), jax.random.fold_in(key_of[9], 1), 0, (4 * E_DEV) - 1).astype(jnp.int32),
        "fault_faces": draw_fault_faces(jax.random.fold_in(key_of[12], 71), 0),
        "slip_flags": plant((jax.random.randint(key_of[11], (FAULTS,), 0, 2) < 1).astype(jnp.int32), jax.random.fold_in(key_of[11], 1), 0, 1),
    }


coarse_dt = 2.0
slip_keep = 0.3


def taylor_terms(rate_level):
    step_size = coarse_dt * jnp.exp2(-rate_level.astype(jnp.float32))
    terms = []
    factor = step_size
    for degree in range(ORDER):
        terms.append(factor)
        factor = factor * step_size / (degree + 2.0)
    return terms


def star_apply(star_matrices, modal):
    return jnp.sum(star_matrices[:, :, :, None, :] * modal[:, :, None, :, :], axis=(0, 1))


def derive(current, star_matrices, stiffness):
    modal = jnp.einsum('dmn,qne->dqme', stiffness, current, precision=lax.Precision.HIGHEST)
    return -star_apply(star_matrices, modal)


def volume_term(integral, star_matrices, stiffness):
    modal = jnp.einsum('dnm,qne->dqme', stiffness, integral, precision=lax.Precision.HIGHEST)
    return star_apply(star_matrices, modal)


def on_faces(field, face_project):
    faces = jnp.einsum('fjn,qne->qjfe', face_project, field, precision=lax.Precision.HIGHEST)
    return faces.reshape(FIELDS * FACE_MODES, -1)


def lift_faces(face_terms, face_project):
    shaped = face_terms.reshape(FIELDS, FACE_MODES, 4, -1)
    return jnp.einsum('fjm,qjfe->qme', face_project, shaped, precision=lax.Precision.HIGHEST)


def apply_flux(matrix, face_terms):
    shaped = face_terms.reshape(FIELDS, FACE_MODES, -1)
    mixed = jnp.einsum('qp,qjx->pjx', matrix, shaped, precision=lax.Precision.HIGHEST)
    return mixed.reshape(FIELDS * FACE_MODES, -1)


def keep_mask(fault_faces, slip_flags, count):
    slide = jnp.zeros((4 * count,), jnp.float32).at[fault_faces].set(slip_flags.astype(jnp.float32))
    fields = jnp.arange(FIELDS)
    shear = ((fields >= 3) & (fields < 6)).astype(jnp.float32)
    keep = 1.0 - (1.0 - slip_keep) * shear[:, None] * slide[None, :]
    return jnp.repeat(keep, FACE_MODES, axis=0)


def local_update(state, star_matrices, stiffness, face_project, flux_inner, flux_outer, rate_level, neighbour, send_slots, fault_faces, slip_flags):
    count = state.shape[-1]
    terms = taylor_terms(rate_level)
    current = state
    integral = terms[0] * state
    outer = jnp.zeros((FIELDS * FACE_MODES, 4 * count), jnp.float32)
    flat_neighbour = neighbour.reshape(-1)
    sent = []
    for degree in range(ORDER):
        if degree > 0:
            current = derive(current, star_matrices, stiffness)
            integral = integral + terms[degree] * current
        faces = on_faces(current, face_project)
        outer = outer + jnp.tile(terms[degree], 4)[None, :] * faces[:, flat_neighbour]
        sent.append(faces[:, send_slots])
    inner = on_faces(integral, face_project)
    keep = keep_mask(fault_faces, slip_flags, count)
    flux = apply_flux(flux_inner, inner) + apply_flux(flux_outer, outer * keep)
    fresh = state + volume_term(integral, star_matrices, stiffness) + lift_faces(flux, face_project)
    return fresh, jnp.stack(sent)


def reference(state, star_matrices, stiffness, face_project, flux_inner, flux_outer, rate_level, neighbour, send_slots, receive_slots, fault_faces, slip_flags):
    devices = N_GX * N_GY
    state_dev = jnp.moveaxis(state.reshape(FIELDS, MODES, devices, E_DEV), 2, 0)
    star_dev = jnp.moveaxis(star_matrices.reshape(3, FIELDS, FIELDS, devices, E_DEV), 3, 0)
    level_dev = rate_level.reshape(devices, E_DEV)
    neighbour_dev = jnp.moveaxis(neighbour.reshape(4, devices, E_DEV), 1, 0)
    send_dev = jnp.moveaxis(send_slots.reshape(4, devices, F_NB), 1, 0)
    receive_dev = jnp.moveaxis(receive_slots.reshape(4, devices, F_NB), 1, 0)
    fault_dev = fault_faces.reshape(devices, FAULT_DEV)
    flags_dev = slip_flags.reshape(devices, FAULT_DEV)

    def first(items):
        return local_update(items[0], items[1], stiffness, face_project, flux_inner, flux_outer, items[2], items[3], items[4], items[5], items[6])

    partial_value, stacks = lax.map(first, (state_dev, star_dev, level_dev, neighbour_dev, send_dev, fault_dev, flags_dev))

    def second(items):
        index, level, receive, fault, flags, fresh = items
        column = index // N_GY
        row = index % N_GY
        sources = [index - N_GY, index + N_GY, index - 1, index + 1]
        valid = [column > 0, column < N_GX - 1, row > 0, row < N_GY - 1]
        target_terms = taylor_terms(level[receive % E_DEV])
        count = level.shape[0]
        accum = jnp.zeros((FIELDS * FACE_MODES, 4 * count), jnp.float32)
        for direction in range(4):
            source = jnp.clip(sources[direction], 0, devices - 1)
            stack = lax.dynamic_index_in_dim(stacks, source, 0, keepdims=False)[:, :, direction, :]
            stack = stack * valid[direction].astype(jnp.float32)
            arrived = target_terms[0][direction][None, :] * stack[0]
            for degree in range(1, ORDER):
                arrived = arrived + target_terms[degree][direction][None, :] * stack[degree]
            accum = accum.at[:, receive[direction]].add(arrived)
        keep = keep_mask(fault, flags, count)
        return fresh + lift_faces(apply_flux(flux_outer, accum * keep), face_project)

    indices = jnp.arange(devices, dtype=jnp.int32)
    final = lax.map(second, (indices, level_dev, receive_dev, fault_dev, flags_dev, partial_value))
    return jnp.moveaxis(final, 0, 2).reshape(FIELDS, MODES, devices * E_DEV)
```

```python
import functools

import jax
import jax.numpy as jnp
from jax import lax
from jax.experimental import pallas as pl
from jax.experimental.pallas import tpu as pltpu
from jax.sharding import PartitionSpec as P

FIELDS = 9
MODES = 56
FACE_MODES = 21
ORDER = 6
LEVELS = 3
COUNT = 128
SLOTS = 256
ROWS = FIELDS * FACE_MODES

coarse_dt = 2.0
slip_keep = 0.3

f32 = jnp.float32
bf16 = jnp.bfloat16


def level_terms(level):
    step = coarse_dt * 2.0**-level
    terms = []
    factor = step
    for degree in range(ORDER):
        terms.append(factor)
        factor = factor * step / (degree + 2.0)
    return terms


def split(value):
    high = value.astype(bf16)
    low = (value - high.astype(f32)).astype(bf16)
    return high, low


def split_f32(value):
    high = value.astype(bf16).astype(f32)
    return high, value - high


def matmul(left, right):
    return jnp.dot(left, right, preferred_element_type=f32)


def matmul_nt(left, right):
    return lax.dot_general(left, right, (((1,), (1,)), ((), ())), preferred_element_type=f32)


def place_triple(ref, row, value):
    rows, cols = value.shape
    high, low = split_f32(value)
    for slot, part in enumerate((high, high, low)):
        ref[row : row + rows, slot * 64 : slot * 64 + cols] = part


def element_hot(faces, count):
    which = lax.broadcasted_iota(jnp.int32, (COUNT, count), 0)
    return jnp.where(which == (faces & (COUNT - 1)), 1.0, 0.0).astype(bf16)


def block_hot(hot, blocks, block):
    mask = jnp.where(blocks == block, 1.0, 0.0)
    return hot * jnp.broadcast_to(mask, hot.shape).astype(bf16)


def pair_row(ref):
    return jnp.concatenate([ref[0:1, :], ref[1:2, :]], axis=1)


def fill_modal(modal, left, pieces):
    for first in range(0, FIELDS * COUNT, 2 * COUNT):
        columns = slice(first, min(first + 2 * COUNT, FIELDS * COUNT))
        right = jnp.concatenate([pieces[:, columns], pieces[0:64, columns]], axis=0)
        modal[:, columns] = matmul(left[...], right)


def mix_star(modal, star, group):
    sums = [None] * len(group)
    for d in range(3):
        for q in range(FIELDS):
            value = modal[d * MODES : (d + 1) * MODES, q * COUNT : (q + 1) * COUNT]
            for at, p in enumerate(group):
                term = star[q, p, d : d + 1, :] * value
                sums[at] = term if sums[at] is None else sums[at] + term
    return sums


def levels_kernel(
    odd, level_in, receive_in, send_in, stiffness_in, faces_in, neighbour_in, fault_in, flags_in, inner_in, outer_in,
    state_in, star_in,
    level, receive, send, stiffness, face_project, neighbour, fault, flags, flux_inner, flux_outer,
    state, star,
    level_a, level_c, want_b, want_d,
    receive_all, send_all, faces_all, inner_all, outer_all, square, sems,
):
    ends = (
        (level_in, level), (receive_in, receive_all), (send_in, send_all), (stiffness_in, stiffness),
        (faces_in, faces_all), (neighbour_in, neighbour), (fault_in, fault), (flags_in, flags), (inner_in, inner_all),
        (outer_in, outer_all), (state_in, state), (star_in, star),
    )
    moves = [pltpu.make_async_copy(source, copy, sems.at[at]) for at, (source, copy) in enumerate(ends)]
    for move in moves:
        move.start()
    odd_x, odd_y = odd[0:1, :] == 1, odd[1:2, :] == 1
    for at in range(3):
        moves[at].wait()
    level_all = jnp.broadcast_to(level[...], (8, COUNT))
    rows = []
    coming = [receive_all[at : at + 1, :] for at in range(4)]
    going = [send_all[at : at + 1, :] for at in range(4)]
    for at, (flip, first) in enumerate(((odd_x, 0), (odd_y, 2))):
        one, other = first, first + 1
        send[at : at + 1, :] = jnp.where(flip, going[other], going[one])
        send[at + 2 : at + 3, :] = jnp.where(flip, going[one], going[other])
        receive[at : at + 1, :] = jnp.where(flip, coming[one], coming[other])
        receive[at + 2 : at + 3, :] = jnp.where(flip, coming[other], coming[one])
    for at in range(4):
        row = receive[at : at + 1, :]
        rows += [row[:, :COUNT], row[:, COUNT:]]
    index = jnp.concatenate(rows, axis=0) & (COUNT - 1)
    found = jnp.take_along_axis(level_all, index, axis=1, mode="promise_in_bounds")
    for at, out in enumerate((level_a, level_c, want_b, want_d)):
        out[...] = found[2 * at : 2 * at + 2, :]
    for at in range(3, 5):
        moves[at].wait()
    for f in range(4):
        face_project[f] = faces_all[:, f, :]
    for at in range(5, 10):
        moves[at].wait()
    for source, spread in ((inner_all, flux_inner), (outer_all, flux_outer)):
        square[...] = jnp.zeros_like(square)
        square[0:FIELDS, 0:FIELDS] = source[...]
        turned = square[...].T
        for q in range(FIELDS):
            spread[q] = jnp.broadcast_to(turned[0:FIELDS, q : q + 1], (FIELDS, COUNT))
    for at in range(10, len(moves)):
        moves[at].wait()


def taylor_kernel(
    state, star, stiffness, face_project, level,
    table, own,
    wide, left, face_left, stack, modal, pieces, level_pieces,
):
    wide[...] = jnp.zeros_like(wide)
    for d in range(3):
        place_triple(wide, d * MODES, -stiffness[d])
    left[...] = wide[0:168, 0:192].astype(bf16)
    wide[0:96, :] = jnp.zeros((96, 256), f32)
    for f in range(4):
        place_triple(wide, f * 24, face_project[f])
    face_left[...] = wide[0:96, 0:192].astype(bf16)
    pieces[...] = jnp.zeros_like(pieces)
    level_pieces[...] = jnp.zeros_like(level_pieces)

    for q in range(FIELDS):
        value = state[q]
        stack[0, q] = value
        high, low = split(value)
        pieces[0:MODES, q * COUNT : (q + 1) * COUNT] = high
        pieces[64 : 64 + MODES, q * COUNT : (q + 1) * COUNT] = low

    def step(degree, carry):
        fill_modal(modal, left, pieces)
        for first in range(0, FIELDS, 3):
            group = range(first, first + 3)
            for p, value in zip(group, mix_star(modal, star, group)):
                stack[degree + 1, p] = value
                high, low = split(value)
                pieces[0:MODES, p * COUNT : (p + 1) * COUNT] = high
                pieces[64 : 64 + MODES, p * COUNT : (p + 1) * COUNT] = low
        return carry

    lax.fori_loop(0, ORDER - 1, step, 0)

    terms = [level_terms(at) for at in range(LEVELS)]
    for q in range(FIELDS):
        sums = [None] * LEVELS
        for degree in range(ORDER):
            value = stack[degree, q]
            for at in range(LEVELS):
                term = terms[at][degree] * value
                sums[at] = term if degree == 0 else sums[at] + term
        own[q] = jnp.where(level[...] == 0, sums[0], jnp.where(level[...] == 1, sums[1], sums[2]))
        for at in range(LEVELS):
            high, low = split(sums[at])
            column = (at * FIELDS + q) * COUNT
            level_pieces[0:MODES, column : column + COUNT] = high
            level_pieces[64 : 64 + MODES, column : column + COUNT] = low

    for at in range(LEVELS):
        columns = slice(at * FIELDS * COUNT, (at + 1) * FIELDS * COUNT)
        right = jnp.concatenate([level_pieces[:, columns], level_pieces[0:64, columns]], axis=0)
        faces = matmul(face_left[...], right)
        for q in range(FIELDS):
            for f in range(4):
                high, low = split_f32(faces[f * 24 : f * 24 + 24, q * COUNT : (q + 1) * COUNT])
                column = (at * 4 + f) * COUNT
                table[q * 48 : q * 48 + 48, column : column + COUNT] = jnp.concatenate(
                    [high, low], axis=0
                ).astype(bf16)


def put(out, found):
    for q in range(FIELDS):
        both = found[q * 48 : q * 48 + 24, :] + found[q * 48 + 24 : q * 48 + 48, :]
        out[q * FACE_MODES : (q + 1) * FACE_MODES, :] = both[:FACE_MODES, :]


def gather_slots(faces, levels, table, out, hot):
    blocks = levels * 4 + (faces >> 7)
    element = element_hot(faces, SLOTS)
    for block in range(12):
        hot[block * COUNT : (block + 1) * COUNT, :] = block_hot(element, blocks, block)
    put(out, matmul(table[...], hot[...]))


def gather_kernel(at, send, levels, table, out, hot):
    gather_slots(send[at : at + 1, :], pair_row(levels), table, out, hot)


def gather_levels_kernel(at, send, table, out, hot):
    faces = send[at : at + 1, :]
    element = element_hot(faces, SLOTS)
    for block in range(4):
        hot[block * COUNT : (block + 1) * COUNT, :] = block_hot(element, faces >> 7, block)
    for level in range(LEVELS):
        put(out.at[level], matmul(table[:, level * 512 : level * 512 + 512], hot[...]))


def face_transposed(square, face_project):
    square[...] = jnp.zeros_like(square)
    for f in range(4):
        square[f * 24 : f * 24 + FACE_MODES, 0:MODES] = face_project[f]
    return square[...].T[0:MODES, 0:96]


def local_kernel(
    flux_inner, state, star, stiffness, face_project, level, neighbour, fault, flags, receive, table, own,
    base, outer, keep, lift_left, arrive_hot,
    square, wide, left, pieces, modal, hot,
):
    projected = face_transposed(square, face_project)
    rows = square[0:96, :]
    high, low = split(projected)
    lift_left[:, 0:96] = high.astype(f32)
    lift_left[:, 96:192] = high.astype(f32)
    lift_left[:, 192:288] = low.astype(f32)
    right_high, right_low = split(rows)
    gram = (
        matmul(high, right_high) + matmul(high, right_low) + matmul(low, right_high)
    )[:, 0:MODES]
    wide[...] = jnp.zeros_like(wide)
    place_triple(wide, 3 * MODES, gram)
    square[...] = jnp.zeros_like(square)
    for d in range(3):
        square[0:MODES, 0:MODES] = stiffness[d]
        place_triple(wide, d * MODES, square[...].T[0:MODES, 0:MODES])
    left[...] = wide[0:224, 0:192].astype(bf16)
    pieces[...] = jnp.zeros_like(pieces)
    for q in range(FIELDS):
        high, low = split(own[q])
        pieces[0:MODES, q * COUNT : (q + 1) * COUNT] = high
        pieces[64 : 64 + MODES, q * COUNT : (q + 1) * COUNT] = low
    fill_modal(modal, left, pieces)
    for first in range(0, FIELDS, 3):
        group = range(first, first + 3)
        sums = mix_star(modal, star, group)
        for q in range(FIELDS):
            value = modal[168:224, q * COUNT : (q + 1) * COUNT]
            for at, p in enumerate(group):
                sums[at] = sums[at] + flux_inner[q, p : p + 1, :] * value
        for at, p in enumerate(group):
            base[p] = state[p] + sums[at]

    for f in range(4):
        faces = neighbour[f : f + 1, :]
        blocks = level[...] * 4 + (faces >> 7)
        element = element_hot(faces, COUNT)
        for block in range(12):
            hot[block * COUNT : (block + 1) * COUNT, f * COUNT : (f + 1) * COUNT] = block_hot(
                element, blocks, block
            )
    found = matmul(table[...], hot[...])
    for q in range(FIELDS):
        outer[q * 24 : q * 24 + 24, :] = found[q * 48 : q * 48 + 24, :] + found[q * 48 + 24 : q * 48 + 48, :]

    which = lax.broadcasted_iota(jnp.int32, (4 * COUNT, fault.shape[1]), 0)
    at_fault = jnp.where(which == fault[...], 1.0, 0.0).astype(bf16)
    slips = jnp.broadcast_to(flags[...].astype(f32), (16, fault.shape[1])).astype(bf16)
    keep[...] = 1.0 - (1.0 - slip_keep) * matmul_nt(slips, at_fault)[0:8, :]

    for at in range(4):
        faces = receive[at : at + 1, :]
        element = element_hot(faces, SLOTS)
        for block in range(4):
            arrive_hot[block * COUNT : (block + 1) * COUNT, at * SLOTS : (at + 1) * SLOTS] = block_hot(
                element, faces >> 7, block
            )


def place_arrived(arrived, at, pick):
    for q in range(FIELDS):
        value = pick(slice(q * FACE_MODES, (q + 1) * FACE_MODES))
        value = jnp.concatenate([value, jnp.zeros((3, SLOTS), f32)], axis=0)
        high, low = split_f32(value)
        arrived[q * 48 : q * 48 + 48, at * SLOTS : (at + 1) * SLOTS] = jnp.concatenate([high, low], axis=0).astype(
            bf16
        )


def picked(levels, arrive, rows):
    return jnp.where(levels == 0, arrive[0, rows, :], jnp.where(levels == 1, arrive[1, rows, :], arrive[2, rows, :]))


def absorb_kernel(level_a, level_c, arrive_a, arrive_c, arrive_hot, outer, total, arrived):
    for at, (level, arrive) in enumerate(((level_a, arrive_a), (level_c, arrive_c))):
        levels = pair_row(level)
        place_arrived(arrived, at, lambda rows: picked(levels, arrive, rows))
    found = matmul_nt(arrived[...], arrive_hot[:, 0:512])
    for q in range(FIELDS):
        total[q * 24 : q * 24 + 24, :] = (
            outer[q * 24 : q * 24 + 24, :] + found[q * 48 : q * 48 + 24, :] + found[q * 48 + 24 : q * 48 + 48, :]
        )


def final_kernel(
    flux_outer, arrive_b, arrive_d, arrive_hot, base, outer, keep, lift_left,
    updated,
    arrived, lifted_right, lifted,
):
    place_arrived(arrived, 0, lambda rows: arrive_b[rows, :])
    place_arrived(arrived, 1, lambda rows: arrive_d[rows, :])
    found = matmul_nt(arrived[...], arrive_hot[:, 512:1024])
    for q in range(FIELDS):
        total = found[q * 48 : q * 48 + 24, :] + found[q * 48 + 24 : q * 48 + 48, :] + outer[q * 24 : q * 24 + 24, :]
        if 3 <= q < 6:
            total = total * keep[0:1, :]
        faces = jnp.concatenate([total[:, f * COUNT : (f + 1) * COUNT] for f in range(4)], axis=0)
        high, low = split(faces)
        columns = slice(q * COUNT, (q + 1) * COUNT)
        lifted_right[0:96, columns] = high
        lifted_right[96:192, columns] = low
        lifted_right[192:288, columns] = high
    left = lift_left[...].astype(bf16)
    for first in range(0, FIELDS * COUNT, 2 * COUNT):
        columns = slice(first, min(first + 2 * COUNT, FIELDS * COUNT))
        lifted[:, columns] = matmul(left, lifted_right[:, columns])
    for first in range(0, FIELDS, 3):
        sums = [base[p] for p in range(first, first + 3)]
        for q in range(FIELDS):
            value = lifted[:, q * COUNT : (q + 1) * COUNT]
            for at in range(3):
                sums[at] = sums[at] + flux_outer[q, first + at : first + at + 1, :] * value
        for at in range(3):
            updated[first + at] = sums[at]


def spec(space=pltpu.VMEM):
    return pl.BlockSpec(memory_space=space)


def call(kernel, outs, scratch, near, values, flops, space=pltpu.VMEM):
    moved = sum(4 * value.size for value in values)
    if space is pltpu.HBM:
        values = [pltpu.with_memory_space_constraint(value, space) for value in values]
    return pl.pallas_call(
        kernel,
        out_shape=outs,
        in_specs=[spec()] * len(near) + [spec(space)] * len(values),
        out_specs=jax.tree.map(lambda _: spec(), outs),
        scratch_shapes=scratch,
        cost_estimate=pl.CostEstimate(flops=flops, bytes_accessed=moved, transcendentals=0),
        compiler_params=pltpu.CompilerParams(vmem_limit_bytes=24 << 20),
    )(*near, *values)


def shape(*dims, dtype=f32):
    return jax.ShapeDtypeStruct(dims, dtype)


def swapped(value, axis, first):
    count = lax.axis_size(axis)
    pairs = []
    for low in range(first, count - 1, 2):
        pairs += [(low, low + 1), (low + 1, low)]
    return lax.ppermute(value, axis, pairs)


def shards(
    state, star_matrices, stiffness, face_project, flux_inner, flux_outer, rate_level, neighbour,
    send_slots, receive_slots, fault_faces, slip_flags,
):
    along = lax.broadcasted_iota(jnp.int32, (8, SLOTS), 0)
    odd = jnp.where(along == 0, lax.axis_index("gx") & 1, lax.axis_index("gy") & 1)
    inputs = (
        rate_level.reshape(1, COUNT), receive_slots, send_slots, stiffness, face_project.transpose(1, 0, 2), neighbour,
        fault_faces.reshape(1, -1), slip_flags.reshape(1, -1), flux_inner, flux_outer, state, star_matrices.transpose(1, 2, 0, 3),
    )
    held = [shape(*value.shape, dtype=value.dtype) for value in inputs]
    held[4] = shape(*face_project.shape)
    held[8] = held[9] = shape(FIELDS, FIELDS, COUNT)
    row = shape(2, COUNT, dtype=jnp.int32)
    level, receive, send, stiffness, face_project, neighbour, fault, flags, *rest = call(
        levels_kernel,
        tuple(held) + (row,) * 4,
        [
            pltpu.VMEM(receive_slots.shape, jnp.int32),
            pltpu.VMEM(send_slots.shape, jnp.int32),
            pltpu.VMEM(inputs[4].shape, f32),
            pltpu.VMEM((FIELDS, FIELDS), f32),
            pltpu.VMEM((FIELDS, FIELDS), f32),
            pltpu.VMEM((128, 128), f32),
            pltpu.SemaphoreType.DMA((len(inputs),)),
        ],
        (odd,), inputs, 1000, pltpu.HBM,
    )
    flux_inner, flux_outer, state, star, level_a, level_c, want_b, want_d = rest
    level_b = swapped(want_b, "gx", 1)
    level_d = swapped(want_d, "gy", 1)

    table, own = call(
        taylor_kernel,
        (shape(FIELDS * 48, LEVELS * 4 * COUNT, dtype=bf16), shape(FIELDS, MODES, COUNT)),
        [
            pltpu.VMEM((224, 256), f32),
            pltpu.VMEM((168, 192), bf16),
            pltpu.VMEM((96, 192), bf16),
            pltpu.VMEM((ORDER, FIELDS, MODES, COUNT), f32),
            pltpu.VMEM((168, FIELDS * COUNT), f32),
            pltpu.VMEM((128, FIELDS * COUNT), bf16),
            pltpu.VMEM((128, LEVELS * FIELDS * COUNT), bf16),
        ],
        (),
        (state, star, stiffness, face_project, level),
        2000000000,
    )
    piece, pieces = shape(ROWS, SLOTS), shape(LEVELS, ROWS, SLOTS)

    def gathered(at, levels):
        return call(
            functools.partial(gather_kernel, at), piece, [pltpu.VMEM((LEVELS * 4 * COUNT, SLOTS), bf16)], (),
            (send, levels, table), 300000000,
        )

    def gathered_levels(at):
        return call(
            functools.partial(gather_levels_kernel, at), pieces, [pltpu.VMEM((4 * COUNT, SLOTS), bf16)], (),
            (send, table), 300000000,
        )

    arrive_b = swapped(gathered(2, level_b), "gx", 1)
    arrive_c = swapped(gathered_levels(1), "gy", 0)
    arrive_d = swapped(gathered(3, level_d), "gy", 1)
    arrive_a = swapped(gathered_levels(0), "gx", 0)

    base, outer, keep, lift_left, arrive_hot = call(
        local_kernel,
        (
            shape(FIELDS, MODES, COUNT), shape(FIELDS * 24, 4 * COUNT), shape(8, 4 * COUNT), shape(MODES, 288),
            shape(4 * COUNT, 4 * SLOTS, dtype=bf16),
        ),
        [
            pltpu.VMEM((128, 128), f32),
            pltpu.VMEM((224, 256), f32),
            pltpu.VMEM((224, 192), bf16),
            pltpu.VMEM((128, FIELDS * COUNT), bf16),
            pltpu.VMEM((224, FIELDS * COUNT), f32),
            pltpu.VMEM((LEVELS * 4 * COUNT, 4 * COUNT), bf16),
        ],
        (),
        (flux_inner, state, star, stiffness, face_project, level, neighbour, fault, flags, receive, table, own),
        1000000000,
    )
    arrived = pltpu.VMEM((FIELDS * 48, 2 * SLOTS), bf16)
    outer = call(
        absorb_kernel, shape(FIELDS * 24, 4 * COUNT), [arrived], (),
        (level_a, level_c, arrive_a, arrive_c, arrive_hot, outer), 300000000,
    )
    return call(
        final_kernel,
        shape(FIELDS, MODES, COUNT),
        [arrived, pltpu.VMEM((288, FIELDS * COUNT), bf16), pltpu.VMEM((MODES, FIELDS * COUNT), f32)],
        (),
        (flux_outer, arrive_b, arrive_d, arrive_hot, base, outer, keep, lift_left),
        500000000,
    )


def solution(mesh):
    placed = (
        P(None, None, ("gx", "gy")),
        P(None, None, None, ("gx", "gy")),
        P(),
        P(),
        P(),
        P(),
        P(("gx", "gy")),
        P(None, ("gx", "gy")),
        P(None, ("gx", "gy")),
        P(None, ("gx", "gy")),
        P(("gx", "gy")),
        P(("gx", "gy")),
    )

    return jax.shard_map(shards, mesh=mesh, in_specs=placed, out_specs=P(None, None, ("gx", "gy")), check_vma=False)
```

```python
import functools

import jax
import jax.numpy as jnp
from jax import lax
from jax.experimental import pallas as pl
from jax.experimental.pallas import tpu as pltpu
from jax.sharding import PartitionSpec as P

FIELDS = 9
MODES = 56
FACE_MODES = 21
ORDER = 6
LEVELS = 3
COUNT = 128
SLOTS = 256
ROWS = FIELDS * FACE_MODES

coarse_dt = 2.0
slip_keep = 0.3

f32 = jnp.float32
bf16 = jnp.bfloat16


def level_terms(level):
    step = coarse_dt * 2.0**-level
    terms = []
    factor = step
    for degree in range(ORDER):
        terms.append(factor)
        factor = factor * step / (degree + 2.0)
    return terms


def split(value):
    high = value.astype(bf16)
    low = (value - high.astype(f32)).astype(bf16)
    return high, low


def split_f32(value):
    high = value.astype(bf16).astype(f32)
    return high, value - high


def matmul(left, right):
    return jnp.dot(left, right, preferred_element_type=f32)


def matmul_nt(left, right):
    return lax.dot_general(left, right, (((1,), (1,)), ((), ())), preferred_element_type=f32)


def place_triple(ref, row, value):
    rows, cols = value.shape
    high, low = split_f32(value)
    for slot, part in enumerate((high, high, low)):
        ref[row : row + rows, slot * 64 : slot * 64 + cols] = part


def element_hot(faces, count):
    which = lax.broadcasted_iota(jnp.int32, (COUNT, count), 0)
    return jnp.where(which == (faces & (COUNT - 1)), 1.0, 0.0).astype(bf16)


def block_hot(hot, blocks, block):
    mask = jnp.where(blocks == block, 1.0, 0.0)
    return hot * jnp.broadcast_to(mask, hot.shape).astype(bf16)


def pair_row(ref):
    return jnp.concatenate([ref[0:1, :], ref[1:2, :]], axis=1)


def fill_modal(modal, left, pieces, first):
    right = jnp.concatenate([pieces[first + at] for at in range(3)], axis=1)
    both = matmul(left[...], jnp.concatenate([right, right[0:64]], axis=0))
    for at in range(3):
        modal[first + at] = both[:, at * COUNT : (at + 1) * COUNT]


def place_pieces(pieces, at, value):
    high, low = split(value)
    pieces[at, 0:MODES, :] = high
    pieces[at, 64 : 64 + MODES, :] = low


def mix_star(modal, star, group):
    sums = [None] * len(group)
    for d in range(3):
        for q in range(FIELDS):
            value = modal[q, d * MODES : (d + 1) * MODES, :]
            for at, p in enumerate(group):
                term = star[q, p, d : d + 1, :] * value
                sums[at] = term if sums[at] is None else sums[at] + term
    return sums


def levels_kernel(
    odd, level_in, receive_in, send_in, stiffness_in, faces_in, neighbour_in, fault_in, flags_in, inner_in, outer_in,
    state_in, star_in,
    level, receive, send, stiffness, face_project, neighbour, fault, flags, flux_inner, flux_outer,
    state, star,
    level_a, level_c, want_b, want_d,
    receive_all, send_all, faces_all, inner_all, outer_all, square, sems,
):
    ends = (
        (level_in, level), (receive_in, receive_all), (send_in, send_all), (stiffness_in, stiffness),
        (faces_in, faces_all), (neighbour_in, neighbour), (fault_in, fault), (flags_in, flags), (inner_in, inner_all),
        (outer_in, outer_all), (state_in, state), (star_in, star),
    )
    moves = [pltpu.make_async_copy(source, copy, sems.at[at]) for at, (source, copy) in enumerate(ends)]
    for move in moves:
        move.start()
    odd_x, odd_y = odd[0:1, :] == 1, odd[1:2, :] == 1
    for at in range(3):
        moves[at].wait()
    level_all = jnp.broadcast_to(level[...], (8, COUNT))
    rows = []
    coming = [receive_all[at : at + 1, :] for at in range(4)]
    going = [send_all[at : at + 1, :] for at in range(4)]
    for at, (flip, first) in enumerate(((odd_x, 0), (odd_y, 2))):
        one, other = first, first + 1
        send[at : at + 1, :] = jnp.where(flip, going[other], going[one])
        send[at + 2 : at + 3, :] = jnp.where(flip, going[one], going[other])
        receive[at : at + 1, :] = jnp.where(flip, coming[one], coming[other])
        receive[at + 2 : at + 3, :] = jnp.where(flip, coming[other], coming[one])
    for at in range(4):
        row = receive[at : at + 1, :]
        rows += [row[:, :COUNT], row[:, COUNT:]]
    index = jnp.concatenate(rows, axis=0) & (COUNT - 1)
    found = jnp.take_along_axis(level_all, index, axis=1, mode="promise_in_bounds")
    for at, out in enumerate((level_a, level_c, want_b, want_d)):
        out[...] = found[2 * at : 2 * at + 2, :]
    for at in range(3, 5):
        moves[at].wait()
    for f in range(4):
        face_project[f] = faces_all[:, f, :]
    for at in range(5, 10):
        moves[at].wait()
    for source, spread in ((inner_all, flux_inner), (outer_all, flux_outer)):
        square[...] = jnp.zeros_like(square)
        square[0:FIELDS, 0:FIELDS] = source[...]
        turned = square[...].T
        for q in range(FIELDS):
            spread[q] = jnp.broadcast_to(turned[0:FIELDS, q : q + 1], (FIELDS, COUNT))
    for at in range(10, len(moves)):
        moves[at].wait()


def taylor_kernel(
    state, star, stiffness, face_project, level,
    table, own,
    wide, left, face_left, stack, modal_even, modal_odd, pieces, level_pieces,
):
    wide[...] = jnp.zeros_like(wide)
    for d in range(3):
        place_triple(wide, d * MODES, -stiffness[d])
    left[...] = wide[0:168, 0:192].astype(bf16)
    wide[0:96, :] = jnp.zeros((96, 256), f32)
    for f in range(4):
        place_triple(wide, f * 24, face_project[f])
    face_left[...] = wide[0:96, 0:192].astype(bf16)
    pieces[...] = jnp.zeros_like(pieces)
    level_pieces[...] = jnp.zeros_like(level_pieces)

    for q in range(FIELDS):
        value = state[q]
        stack[0, q] = value
        place_pieces(pieces, q, value)

    def step(degree, carry):
        for first in range(0, FIELDS, 3):
            fill_modal(modal_even, left, pieces, first)
        for first in range(0, FIELDS, 3):
            group = range(first, first + 3)
            for p, value in zip(group, mix_star(modal_even, star, group)):
                stack[degree + 1, p] = value
                place_pieces(pieces, p, value)
        return carry

    lax.fori_loop(0, ORDER - 1, step, 0)

    terms = [level_terms(at) for at in range(LEVELS)]
    for q in range(FIELDS):
        sums = [None] * LEVELS
        for degree in range(ORDER):
            value = stack[degree, q]
            for at in range(LEVELS):
                term = terms[at][degree] * value
                sums[at] = term if degree == 0 else sums[at] + term
        own[q] = jnp.where(level[...] == 0, sums[0], jnp.where(level[...] == 1, sums[1], sums[2]))
        for at in range(LEVELS):
            high, low = split(sums[at])
            column = (at * FIELDS + q) * COUNT
            level_pieces[0:MODES, column : column + COUNT] = high
            level_pieces[64 : 64 + MODES, column : column + COUNT] = low

    for at in range(LEVELS):
        columns = slice(at * FIELDS * COUNT, (at + 1) * FIELDS * COUNT)
        right = jnp.concatenate([level_pieces[:, columns], level_pieces[0:64, columns]], axis=0)
        faces = matmul(face_left[...], right)
        for q in range(FIELDS):
            for f in range(4):
                high, low = split_f32(faces[f * 24 : f * 24 + 24, q * COUNT : (q + 1) * COUNT])
                column = (at * 4 + f) * COUNT
                table[q * 48 : q * 48 + 48, column : column + COUNT] = jnp.concatenate(
                    [high, low], axis=0
                ).astype(bf16)


def starts_early():
    return lax.rem(lax.axis_index("gx"), 8) == 0


def taylor_early_kernel(*refs):
    @pl.when(starts_early())
    def _():
        taylor_kernel(*refs)


def taylor_late_kernel(*refs):
    @pl.when(jnp.logical_not(starts_early()))
    def _():
        taylor_kernel(*refs[:5], *refs[7:])

    @pl.when(starts_early())
    def _():
        refs[7][...] = refs[5][...]
        refs[8][...] = refs[6][...]


def put(out, found):
    for q in range(FIELDS):
        both = found[q * 48 : q * 48 + 24, :] + found[q * 48 + 24 : q * 48 + 48, :]
        out[q * FACE_MODES : (q + 1) * FACE_MODES, :] = both[:FACE_MODES, :]


def gather_slots(faces, levels, table, out, hot):
    blocks = levels * 4 + (faces >> 7)
    element = element_hot(faces, SLOTS)
    for block in range(12):
        hot[block * COUNT : (block + 1) * COUNT, :] = block_hot(element, blocks, block)
    put(out, matmul(table[...], hot[...]))


def gather_kernel(at, send, levels, table, out, hot):
    gather_slots(send[at : at + 1, :], pair_row(levels), table, out, hot)


def gather_levels_kernel(at, send, table, out, hot):
    faces = send[at : at + 1, :]
    element = element_hot(faces, SLOTS)
    for block in range(4):
        hot[block * COUNT : (block + 1) * COUNT, :] = block_hot(element, faces >> 7, block)
    for level in range(LEVELS):
        put(out.at[level], matmul(table[:, level * 512 : level * 512 + 512], hot[...]))


def face_transposed(square, face_project):
    square[...] = jnp.zeros_like(square)
    for f in range(4):
        square[f * 24 : f * 24 + FACE_MODES, 0:MODES] = face_project[f]
    return square[...].T[0:MODES, 0:96]


def local_kernel(
    flux_inner, state, star, stiffness, face_project, level, neighbour, fault, flags, receive, table, own,
    base, outer, keep, lift_left, arrive_hot,
    square, wide, left, pieces, modal, hot,
):
    projected = face_transposed(square, face_project)
    rows = square[0:96, :]
    high, low = split(projected)
    lift_left[:, 0:96] = high.astype(f32)
    lift_left[:, 96:192] = high.astype(f32)
    lift_left[:, 192:288] = low.astype(f32)
    right_high, right_low = split(rows)
    gram = (
        matmul(high, right_high) + matmul(high, right_low) + matmul(low, right_high)
    )[:, 0:MODES]
    wide[...] = jnp.zeros_like(wide)
    place_triple(wide, 3 * MODES, gram)
    square[...] = jnp.zeros_like(square)
    for d in range(3):
        square[0:MODES, 0:MODES] = stiffness[d]
        place_triple(wide, d * MODES, square[...].T[0:MODES, 0:MODES])
    left[...] = wide[0:224, 0:192].astype(bf16)
    pieces[...] = jnp.zeros_like(pieces)
    for q in range(FIELDS):
        place_pieces(pieces, q, own[q])
    for first in range(0, FIELDS, 3):
        fill_modal(modal, left, pieces, first)
    for first in range(0, FIELDS, 3):
        group = range(first, first + 3)
        sums = mix_star(modal, star, group)
        for q in range(FIELDS):
            value = modal[q, 168:224, :]
            for at, p in enumerate(group):
                sums[at] = sums[at] + flux_inner[q, p : p + 1, :] * value
        for at, p in enumerate(group):
            base[p] = state[p] + sums[at]

    for f in range(4):
        faces = neighbour[f : f + 1, :]
        blocks = level[...] * 4 + (faces >> 7)
        element = element_hot(faces, COUNT)
        for block in range(12):
            hot[block * COUNT : (block + 1) * COUNT, f * COUNT : (f + 1) * COUNT] = block_hot(
                element, blocks, block
            )
    found = matmul(table[...], hot[...])
    for q in range(FIELDS):
        outer[q * 24 : q * 24 + 24, :] = found[q * 48 : q * 48 + 24, :] + found[q * 48 + 24 : q * 48 + 48, :]

    which = lax.broadcasted_iota(jnp.int32, (4 * COUNT, fault.shape[1]), 0)
    at_fault = jnp.where(which == fault[...], 1.0, 0.0).astype(bf16)
    slips = jnp.broadcast_to(flags[...].astype(f32), (16, fault.shape[1])).astype(bf16)
    keep[...] = 1.0 - (1.0 - slip_keep) * matmul_nt(slips, at_fault)[0:8, :]

    for at in range(4):
        faces = receive[at : at + 1, :]
        element = element_hot(faces, SLOTS)
        for block in range(4):
            arrive_hot[block * COUNT : (block + 1) * COUNT, at * SLOTS : (at + 1) * SLOTS] = block_hot(
                element, faces >> 7, block
            )


def place_arrived(arrived, at, pick):
    for q in range(FIELDS):
        value = pick(slice(q * FACE_MODES, (q + 1) * FACE_MODES))
        value = jnp.concatenate([value, jnp.zeros((3, SLOTS), f32)], axis=0)
        high, low = split_f32(value)
        arrived[q * 48 : q * 48 + 48, at * SLOTS : (at + 1) * SLOTS] = jnp.concatenate([high, low], axis=0).astype(
            bf16
        )


def picked(levels, arrive, rows):
    return jnp.where(levels == 0, arrive[0, rows, :], jnp.where(levels == 1, arrive[1, rows, :], arrive[2, rows, :]))


def absorb_kernel(level_a, level_c, arrive_a, arrive_c, arrive_b, arrive_hot, outer, total, arrived):
    for at, (level, arrive) in enumerate(((level_a, arrive_a), (level_c, arrive_c))):
        levels = pair_row(level)
        place_arrived(arrived, at, lambda rows: picked(levels, arrive, rows))
    place_arrived(arrived, 2, lambda rows: arrive_b[rows, :])
    found = matmul_nt(arrived[...], arrive_hot[:, 0:768])
    for q in range(FIELDS):
        total[q * 24 : q * 24 + 24, :] = (
            outer[q * 24 : q * 24 + 24, :] + found[q * 48 : q * 48 + 24, :] + found[q * 48 + 24 : q * 48 + 48, :]
        )


def final_kernel(
    flux_outer, arrive_d, arrive_hot, base, outer, keep, lift_left,
    updated,
    arrived, lifted_right, lifted,
):
    place_arrived(arrived, 0, lambda rows: arrive_d[rows, :])
    found = matmul_nt(arrived[...], arrive_hot[:, 768:1024])
    for q in range(FIELDS):
        total = found[q * 48 : q * 48 + 24, :] + found[q * 48 + 24 : q * 48 + 48, :] + outer[q * 24 : q * 24 + 24, :]
        if 3 <= q < 6:
            total = total * keep[0:1, :]
        faces = jnp.concatenate([total[:, f * COUNT : (f + 1) * COUNT] for f in range(4)], axis=0)
        high, low = split(faces)
        columns = slice(q * COUNT, (q + 1) * COUNT)
        lifted_right[0:96, columns] = high
        lifted_right[96:192, columns] = low
        lifted_right[192:288, columns] = high
    left = lift_left[...].astype(bf16)
    for first in range(0, FIELDS * COUNT, 2 * COUNT):
        columns = slice(first, min(first + 2 * COUNT, FIELDS * COUNT))
        lifted[:, columns] = matmul(left, lifted_right[:, columns])
    for first in range(0, FIELDS, 3):
        sums = [base[p] for p in range(first, first + 3)]
        for q in range(FIELDS):
            value = lifted[:, q * COUNT : (q + 1) * COUNT]
            for at in range(3):
                sums[at] = sums[at] + flux_outer[q, first + at : first + at + 1, :] * value
        for at in range(3):
            updated[first + at] = sums[at]


def spec(space=pltpu.VMEM):
    return pl.BlockSpec(memory_space=space)


def call(kernel, outs, scratch, near, values, flops, space=pltpu.VMEM):
    moved = sum(4 * value.size for value in values)
    if space is pltpu.HBM:
        values = [pltpu.with_memory_space_constraint(value, space) for value in values]
    return pl.pallas_call(
        kernel,
        out_shape=outs,
        in_specs=[spec()] * len(near) + [spec(space)] * len(values),
        out_specs=jax.tree.map(lambda _: spec(), outs),
        scratch_shapes=scratch,
        cost_estimate=pl.CostEstimate(flops=flops, bytes_accessed=moved, transcendentals=0),
        compiler_params=pltpu.CompilerParams(vmem_limit_bytes=24 << 20),
    )(*near, *values)


def shape(*dims, dtype=f32):
    return jax.ShapeDtypeStruct(dims, dtype)


def swapped(value, axis, first):
    count = lax.axis_size(axis)
    pairs = []
    for low in range(first, count - 1, 2):
        pairs += [(low, low + 1), (low + 1, low)]
    return lax.ppermute(value, axis, pairs)


def shards(
    state, star_matrices, stiffness, face_project, flux_inner, flux_outer, rate_level, neighbour,
    send_slots, receive_slots, fault_faces, slip_flags,
):
    along = lax.broadcasted_iota(jnp.int32, (8, SLOTS), 0)
    odd = jnp.where(along == 0, lax.axis_index("gx") & 1, lax.axis_index("gy") & 1)
    inputs = (
        rate_level.reshape(1, COUNT), receive_slots, send_slots, stiffness, face_project.transpose(1, 0, 2), neighbour,
        fault_faces.reshape(1, -1), slip_flags.reshape(1, -1), flux_inner, flux_outer, state, star_matrices.transpose(1, 2, 0, 3),
    )
    held = [shape(*value.shape, dtype=value.dtype) for value in inputs]
    held[4] = shape(*face_project.shape)
    held[8] = held[9] = shape(FIELDS, FIELDS, COUNT)
    row = shape(2, COUNT, dtype=jnp.int32)
    level, receive, send, stiffness, face_project, neighbour, fault, flags, *rest = call(
        levels_kernel,
        tuple(held) + (row,) * 4,
        [
            pltpu.VMEM(receive_slots.shape, jnp.int32),
            pltpu.VMEM(send_slots.shape, jnp.int32),
            pltpu.VMEM(inputs[4].shape, f32),
            pltpu.VMEM((FIELDS, FIELDS), f32),
            pltpu.VMEM((FIELDS, FIELDS), f32),
            pltpu.VMEM((128, 128), f32),
            pltpu.SemaphoreType.DMA((len(inputs),)),
        ],
        (odd,), inputs, 1000, pltpu.HBM,
    )
    flux_inner, flux_outer, state, star, level_a, level_c, want_b, want_d = rest
    taylor_outs = (shape(FIELDS * 48, LEVELS * 4 * COUNT, dtype=bf16), shape(FIELDS, MODES, COUNT))
    taylor_scratch = [
        pltpu.VMEM((224, 256), f32),
        pltpu.VMEM((168, 192), bf16),
        pltpu.VMEM((96, 192), bf16),
        pltpu.VMEM((ORDER, FIELDS, MODES, COUNT), f32),
        pltpu.VMEM((FIELDS, 168, COUNT), f32),
        pltpu.VMEM((FIELDS, 168, COUNT), f32),
        pltpu.VMEM((FIELDS, 128, COUNT), bf16),
        pltpu.VMEM((128, LEVELS * FIELDS * COUNT), bf16),
    ]
    taylor_inputs = (state, star, stiffness, face_project, level)
    early = call(taylor_early_kernel, taylor_outs, taylor_scratch, (), taylor_inputs, 2000000000)
    level_b = swapped(want_b, "gx", 1)
    level_d = swapped(want_d, "gy", 1)

    table, own = call(taylor_late_kernel, taylor_outs, taylor_scratch, (), taylor_inputs + tuple(early), 2000000000)
    piece, pieces = shape(ROWS, SLOTS), shape(LEVELS, ROWS, SLOTS)

    def gathered(at, levels):
        return call(
            functools.partial(gather_kernel, at), piece, [pltpu.VMEM((LEVELS * 4 * COUNT, SLOTS), bf16)], (),
            (send, levels, table), 300000000,
        )

    def gathered_levels(at):
        return call(
            functools.partial(gather_levels_kernel, at), pieces, [pltpu.VMEM((4 * COUNT, SLOTS), bf16)], (),
            (send, table), 300000000,
        )

    arrive_b = swapped(gathered(2, level_b), "gx", 1)
    arrive_c = swapped(gathered_levels(1), "gy", 0)
    arrive_d = swapped(gathered(3, level_d), "gy", 1)
    arrive_a = swapped(gathered_levels(0), "gx", 0)

    base, outer, keep, lift_left, arrive_hot = call(
        local_kernel,
        (
            shape(FIELDS, MODES, COUNT), shape(FIELDS * 24, 4 * COUNT), shape(8, 4 * COUNT), shape(MODES, 288),
            shape(4 * COUNT, 4 * SLOTS, dtype=bf16),
        ),
        [
            pltpu.VMEM((128, 128), f32),
            pltpu.VMEM((224, 256), f32),
            pltpu.VMEM((224, 192), bf16),
            pltpu.VMEM((FIELDS, 128, COUNT), bf16),
            pltpu.VMEM((FIELDS, 224, COUNT), f32),
            pltpu.VMEM((LEVELS * 4 * COUNT, 4 * COUNT), bf16),
        ],
        (),
        (flux_inner, state, star, stiffness, face_project, level, neighbour, fault, flags, receive, table, own),
        1000000000,
    )
    outer = call(
        absorb_kernel, shape(FIELDS * 24, 4 * COUNT), [pltpu.VMEM((FIELDS * 48, 3 * SLOTS), bf16)], (),
        (level_a, level_c, arrive_a, arrive_c, arrive_b, arrive_hot, outer), 300000000,
    )
    return call(
        final_kernel,
        shape(FIELDS, MODES, COUNT),
        [pltpu.VMEM((FIELDS * 48, SLOTS), bf16), pltpu.VMEM((288, FIELDS * COUNT), bf16), pltpu.VMEM((MODES, FIELDS * COUNT), f32)],
        (),
        (flux_outer, arrive_d, arrive_hot, base, outer, keep, lift_left),
        500000000,
    )


def solution(mesh):
    placed = (
        P(None, None, ("gx", "gy")),
        P(None, None, None, ("gx", "gy")),
        P(),
        P(),
        P(),
        P(),
        P(("gx", "gy")),
        P(None, ("gx", "gy")),
        P(None, ("gx", "gy")),
        P(None, ("gx", "gy")),
        P(("gx", "gy")),
        P(("gx", "gy")),
    )

    return jax.shard_map(shards, mesh=mesh, in_specs=placed, out_specs=P(None, None, ("gx", "gy")), check_vma=False)
```
